32 devices in a mesh: dp: 4 (over z), seq: 8 (over y, x, core).
Axes of the slice: x: 2, y: 2, z: 4, core: 2. Of those that a mesh axis runs over, the one named last changes fastest.
Arguments:
- saved_codes: bfloat16 [4, 1024, 1536], P('dp', 'seq'), may hold values from -6 to 6
- code_scales: float32 [4, 12, 1024], P('dp', None, 'seq'), may hold values from 0.25 to 4
- lengths: int32 [4], replicated, may hold values from 128 to 1024, as said below
- in_weight: bfloat16 [3072, 1536], P('dp'), may hold values from -0.15625 to 0.15625
- conv_kernel: float32 [31, 1536], replicated, may hold values from -1 to 1
- bn_gain: float32 [1536], replicated, may hold values from 0.1 to 1.9
- bn_shift: float32 [1536], replicated, may hold values from -3 to 3
- out_grad: bfloat16 [4, 1024, 1536], P('dp', 'seq'), may hold values from -6 to 6
Outputs:
- in_grad: bfloat16 [4, 1024, 1536], P('dp', 'seq')
- weight_grad: float32 [3072, 1536], P('dp')
- kernel_grad: float32 [31, 1536], replicated
- gain_grad: float32 [1536], replicated
- shift_grad: float32 [1536], replicated
The draws below stay inside these ranges and needn't reach their ends.
Inputs may be any that keep to these rules, and one draw needn't show every extreme that they name: `lengths`: at least one recording has exactly 1024 valid frames.
All inputs are finite; a program needn't handle non-finite values.
Results may differ from the reference program's by a relative error of at most 0.0067.
Values may be sent and summed in bfloat16 or wider, within the bound.
A program may use at most 128 MiB of HBM per device.

```python
import math
import jax
import jax.numpy as jnp
from jax import lax

D = 1536
KERNEL = 31
GROUPS = 4
FRAMES = 1024


def draw_lengths(key, part):
    first_key, second_key = jax.random.split(jax.random.fold_in(key, 11))
    cubes = jax.random.randint(first_key, (GROUPS,), 0, 16)
    drawn = FRAMES // 8 + (FRAMES - FRAMES // 8) * (cubes * cubes * cubes) // 3375
    longest = jax.random.randint(second_key, (), 0, GROUPS)
    return jnp.where(jnp.arange(GROUPS) == longest, FRAMES, drawn).astype(jnp.int32)


def levels(own_key, extent, cuts, smallest, largest):
    factor_of, own = 1.0, jax.random.fold_in(own_key, 6)
    for axis_at, shards_of in cuts:
        draws = jnp.exp(jax.random.uniform(jax.random.fold_in(own, axis_at), (shards_of,), jnp.float32, smallest / len(cuts), largest / len(cuts)))
        factor_of = factor_of * jnp.repeat(draws, extent[axis_at] // shards_of).reshape([-1 if axis == axis_at else 1 for axis in range(len(extent))])
    return factor_of


def centred(rng, extent, deviation, reach, shards=(), held_as=jnp.bfloat16):
    result = jax.random.normal(rng, extent, jnp.float32) * deviation
    if len(shards) > 0:
        result = levels(rng, extent, shards, -0.22, 0.18) * result
    return jnp.clip(result, min=-reach, max=reach).astype(held_as)


def setup_inputs(seed: int = 0) -> dict:
    key_list = jax.random.split(jax.random.key(seed), 9)
    saved_codes = centred(key_list[0], (GROUPS, FRAMES, D), 1.0, 6.0, ((0, 4), (1, 8)))
    code_scales = jnp.clip(jnp.exp(math.log(4.0) - 2.7725887 * jax.random.uniform(key_list[1], (GROUPS, D // 128, FRAMES), jnp.float32) ** levels(key_list[1], (GROUPS, D // 128, FRAMES), ((0, 4), (2, 8)), -0.2, 0.2)), 0.25, 4.0)
    lengths = draw_lengths(jax.random.fold_in(key_list[8], 71), 0)
    in_weight = centred(key_list[3], (2 * D, D), D ** -0.5, 0.15625, ((0, 4),))
    conv_kernel = centred(key_list[4], (KERNEL, D), KERNEL ** -0.5, 1.0, (), jnp.float32)
    bn_gain = jnp.clip(1.0 + 0.18 * jax.random.normal(key_list[5], (D,), jnp.float32), 0.1, 1.9)
    bn_shift = centred(key_list[6], (D,), 0.5, 3.0, (), jnp.float32)
    out_grad = centred(key_list[7], (GROUPS, FRAMES, D), 1.0, 6.0, ((0, 4), (1, 8)))
    return dict(saved_codes=saved_codes, code_scales=code_scales, lengths=lengths, in_weight=in_weight, conv_kernel=conv_kernel, bn_gain=bn_gain, bn_shift=bn_shift, out_grad=out_grad)


EPS = 1e-05

def restore(quantized, scales):
    per_channel = jnp.repeat(scales.T, 128, axis=1)
    return (quantized.astype(jnp.float32) * per_channel).astype(jnp.bfloat16)

def depthwise(padded, kernel, frames):
    running = jnp.zeros((frames, padded.shape[1]), jnp.float32)
    for offset in range(kernel.shape[0]):
        running = running + kernel[offset] * padded[offset:offset + frames].astype(jnp.float32)
    return running

def reference(saved_codes, code_scales, lengths, in_weight, conv_kernel, bn_gain, bn_shift, out_grad):
    frames = saved_codes.shape[1]
    feature_width = saved_codes.shape[2]
    tap_count = conv_kernel.shape[0]
    half_span = (tap_count - 1) // 2
    positions = jnp.arange(frames, dtype=jnp.int32)
    counted = jnp.sum(lengths).astype(jnp.float32)
    flipped = conv_kernel[::-1]

    def forward_group(inputs):
        quantized, scales, length = inputs
        valid_mask = (positions < length).astype(jnp.float32)[:, None]
        restored = restore(quantized, scales)
        pre_act = lax.dot_general(restored, in_weight, (((1,), (1,)), ((), ())), preferred_element_type=jnp.float32)
        gated = (pre_act[:, :feature_width] * jax.nn.sigmoid(pre_act[:, feature_width:]) * valid_mask).astype(jnp.bfloat16)
        padded = jnp.pad(gated, ((half_span, half_span), (0, 0)))
        return (pre_act, gated, depthwise(padded, conv_kernel, frames))
    pre_all, gated_all, conv_all = lax.map(forward_group, (saved_codes, code_scales, lengths))
    mask_all = (positions[None, :] < lengths[:, None]).astype(jnp.float32)[:, :, None]
    mean_value = lax.optimization_barrier(jnp.sum(conv_all * mask_all, axis=(0, 1))) / counted
    centered = (conv_all - mean_value) * mask_all
    variance = lax.optimization_barrier(jnp.sum(centered * centered, axis=(0, 1))) / counted
    inverse = lax.rsqrt(variance + EPS)

    def shaped_grad(conv_out, upstream, valid_mask):
        normed = (conv_out - mean_value) * inverse
        shaped = bn_gain * normed + bn_shift
        smooth = jax.nn.sigmoid(shaped)
        grad_shaped = upstream.astype(jnp.float32) * valid_mask * smooth * (1.0 + shaped * (1.0 - smooth))
        return (normed, grad_shaped)

    def sums_group(inputs):
        conv_out, upstream, length = inputs
        valid_mask = (positions < length).astype(jnp.float32)[:, None]
        normed, grad_shaped = shaped_grad(conv_out, upstream, valid_mask)
        return (lax.optimization_barrier(jnp.sum(grad_shaped, axis=0)), lax.optimization_barrier(jnp.sum(grad_shaped * normed, axis=0)))
    shift_parts, gain_parts = lax.map(sums_group, (conv_all, out_grad, lengths))
    shift_grad = lax.optimization_barrier(jnp.sum(shift_parts, axis=0))
    gain_grad = lax.optimization_barrier(jnp.sum(gain_parts, axis=0))

    def backward_group(inputs):
        pre_act, gated, conv_out, quantized, scales, length, upstream = inputs
        valid_mask = (positions < length).astype(jnp.float32)[:, None]
        restored = restore(quantized, scales)
        normed, grad_shaped = shaped_grad(conv_out, upstream, valid_mask)
        grad_conv = bn_gain * inverse * (grad_shaped - (shift_grad + normed * gain_grad) / counted) * valid_mask
        gated_pad = jnp.pad(gated, ((half_span, half_span), (0, 0)))
        kernel_part = jnp.stack([lax.optimization_barrier(jnp.sum(grad_conv * gated_pad[offset:offset + frames].astype(jnp.float32), axis=0)) for offset in range(tap_count)])
        grad_pad = jnp.pad(grad_conv, ((half_span, half_span), (0, 0)))
        grad_gated = depthwise(grad_pad, flipped, frames) * valid_mask
        linear = pre_act[:, :feature_width]
        gate_part = jax.nn.sigmoid(pre_act[:, feature_width:])
        grad_pre = jnp.concatenate([grad_gated * gate_part, grad_gated * linear * gate_part * (1.0 - gate_part)], axis=1).astype(jnp.bfloat16)
        in_grad = jnp.dot(grad_pre, in_weight, preferred_element_type=jnp.float32).astype(jnp.bfloat16)
        weight_part = lax.dot_general(grad_pre, restored, (((0,), (0,)), ((), ())), preferred_element_type=jnp.float32)
        return (in_grad, kernel_part, weight_part)
    in_grad, kernel_parts, weight_parts = lax.map(backward_group, (pre_all, gated_all, conv_all, saved_codes, code_scales, lengths, out_grad))
    return (in_grad, lax.optimization_barrier(jnp.sum(weight_parts, axis=0)), lax.optimization_barrier(jnp.sum(kernel_parts, axis=0)), gain_grad, shift_grad)
```

```python
import functools

import jax
import jax.numpy as jnp
from jax import lax
from jax.experimental import pallas as pl
from jax.experimental.pallas import tpu as pltpu
from jax.sharding import PartitionSpec as P

EPS = 1e-05
MESH = pl.DeviceIdType.MESH
VM = pl.BlockSpec(memory_space=pltpu.VMEM)


def at(d, s):
    return {"dp": d, "seq": s}


def greet(peers):
    barrier = pltpu.get_barrier_semaphore()
    for peer in peers:
        pl.semaphore_signal(barrier, inc=1, device_id=peer, device_id_type=MESH)
    pl.semaphore_wait(barrier, len(peers))


def remote(src, dst, send, recv, peer):
    return pltpu.make_async_remote_copy(
        src_ref=src, dst_ref=dst, send_sem=send, recv_sem=recv, device_id=peer, device_id_type=MESH
    )


def ring_peers(me, count):
    return [lax.rem(me + k, count) for k in range(1, count)]


def merge(parts, stats):
    if not stats:
        return functools.reduce(lambda a, b: a + b, parts)
    sums = [part[0:16] for part in parts]
    squares = [part[16:32] for part in parts]
    counts = [part[32:48] for part in parts]
    total = functools.reduce(lambda a, b: a + b, sums)
    count = functools.reduce(lambda a, b: a + b, counts)
    mean = total / jnp.maximum(count, 1.0)
    spread = functools.reduce(lambda a, b: a + b, squares)
    for own, n in zip(sums, counts):
        shift = own / jnp.maximum(n, 1.0) - mean
        spread = spread + n * (shift * shift)
    return jnp.concatenate([total, spread, count], axis=0)


def sum_kernel(stats, dp_n, seq_n, x_ref, o_ref, near, far, mid, s1, r1, s2, r2):
    d, s = lax.axis_index("dp"), lax.axis_index("seq")
    plane = ring_peers(s, seq_n)
    line = ring_peers(d, dp_n)
    greet([at(d, j) for j in plane] + [at(j, s) for j in line])
    for k, j in enumerate(plane):
        remote(x_ref, near.at[s], s1.at[k], r1.at[s], at(d, j)).start()
    near[s] = x_ref[...]
    for k, j in enumerate(plane):
        copy = remote(x_ref, near.at[j], s1.at[k], r1.at[j], at(d, j))
        copy.wait_recv()
        copy.wait_send()
    mid[...] = merge([near[j] for j in range(seq_n)], stats)
    for k, j in enumerate(line):
        remote(mid, far.at[d], s2.at[k], r2.at[d], at(j, s)).start()
    far[d] = mid[...]
    for k, j in enumerate(line):
        copy = remote(mid, far.at[j], s2.at[k], r2.at[j], at(j, s))
        copy.wait_recv()
        copy.wait_send()
    o_ref[...] = merge([far[j] for j in range(dp_n)], stats)


def sum_all(vectors, stats, collective_id):
    dp_n, seq_n = lax.axis_size("dp"), lax.axis_size("seq")
    blocks = vectors[0].shape[-1] // 128
    stacked = jnp.stack([v.reshape(blocks, 128) for v in vectors])
    stacked = jnp.pad(stacked, ((0, 0), (0, 16 - blocks), (0, 0)))
    rows = 16 * len(vectors)
    shape = (rows, 128)
    out = pl.pallas_call(
        functools.partial(sum_kernel, stats, dp_n, seq_n),
        out_shape=jax.ShapeDtypeStruct(shape, jnp.float32),
        in_specs=[VM],
        out_specs=VM,
        scratch_shapes=[
            pltpu.VMEM((seq_n,) + shape, jnp.float32),
            pltpu.VMEM((dp_n,) + shape, jnp.float32),
            pltpu.VMEM(shape, jnp.float32),
            pltpu.SemaphoreType.DMA((seq_n,)),
            pltpu.SemaphoreType.DMA((seq_n,)),
            pltpu.SemaphoreType.DMA((dp_n,)),
            pltpu.SemaphoreType.DMA((dp_n,)),
        ],
        compiler_params=pltpu.CompilerParams(collective_id=collective_id, has_side_effects=True),
    )(stacked.reshape(shape))
    return out.reshape(len(vectors), 16, 128)[:, :blocks].reshape(len(vectors), blocks * 128)


def square_at(s):
    c, x, y = lax.rem(s, 2), lax.rem(s // 2, 2), s // 4
    sx = (y * 2 + (1 - x)) * 2 + c
    sy = ((1 - y) * 2 + x) * 2 + c
    sd = ((1 - y) * 2 + (1 - x)) * 2 + c
    sc = (y * 2 + x) * 2 + (1 - c)
    return c, x, y, sx, sy, sd, sc


def weights_kernel(w_ref, out, local, zs, zr, xs, xr, ys, yr, fs, fr, cs, cr):
    d, s = lax.axis_index("dp"), lax.axis_index("seq")
    c, x, y, sx, sy, sd, sc = square_at(s)
    rows = w_ref.shape[1]
    half = rows // 2
    low, high = pl.ds(0, half), pl.ds(half, half)
    line = [d + 1 - 2 * lax.rem(d, 2), 2 - d // 2, 3 - 3 * (d // 2)]
    px, py, pc = at(d, sx), at(d, sy), at(d, sc)
    greet([at(j, s) for j in line] + [px, py, pc])
    for k, j in enumerate(line):
        remote(w_ref.at[s], out.at[d, s], zs.at[k], zr.at[d], at(j, s)).start()
    own = pltpu.make_async_copy(w_ref, out.at[d], local)
    own.start()
    pending = []
    core = []

    def to_core(k, n, ref, other):
        copy = remote(ref, ref, cs.at[k, n], cr.at[k, n], pc)
        copy.start()
        pending.append(copy)
        core.append(remote(other, other, cs.at[k, n], cr.at[k, n], pc))

    cx, cy, cd = sx + 1 - 2 * c, sy + 1 - 2 * c, sd + 1 - 2 * c
    for k, j in enumerate(line):
        mine = out.at[j, s]
        remote(mine, mine, zs.at[k], zr.at[j], at(j, s)).wait_recv()
        for send, recv, peer in ((xs, xr, px), (ys, yr, py)):
            copy = remote(mine, mine, send.at[k], recv.at[k], peer)
            copy.start()
            pending.append(copy)
        to_core(k, 0, mine, out.at[j, sc])
    for k, j in enumerate(line):
        remote(out.at[j, sx], out.at[j, sx], xs.at[k], xr.at[k], px).wait_recv()
        part = out.at[j, sx, low]
        copy = remote(part, part, fs.at[k, 0], fr.at[k, 0], py)
        copy.start()
        pending.append(copy)
        to_core(k, 1, out.at[j, sx], out.at[j, cx])
        remote(out.at[j, sy], out.at[j, sy], ys.at[k], yr.at[k], py).wait_recv()
        part = out.at[j, sy, high]
        copy = remote(part, part, fs.at[k, 1], fr.at[k, 1], px)
        copy.start()
        pending.append(copy)
        to_core(k, 2, out.at[j, sy], out.at[j, cy])
    for k, j in enumerate(line):
        part = out.at[j, sd, low]
        remote(part, part, fs.at[k, 0], fr.at[k, 0], py).wait_recv()
        to_core(k, 3, part, out.at[j, cd, low])
        part = out.at[j, sd, high]
        remote(part, part, fs.at[k, 1], fr.at[k, 1], px).wait_recv()
        to_core(k, 4, part, out.at[j, cd, high])
    for copy in core:
        copy.wait_recv()
    for copy in pending:
        copy.wait_send()
    for k, j in enumerate(line):
        remote(w_ref.at[s], out.at[d, s], zs.at[k], zr.at[d], at(j, s)).wait_send()
    own.wait()


def gather_weights(in_weight):
    dp_n, seq_n = lax.axis_size("dp"), lax.axis_size("seq")
    rows, width = in_weight.shape
    dma = pltpu.SemaphoreType.DMA
    out = pl.pallas_call(
        weights_kernel,
        out_shape=jax.ShapeDtypeStruct((dp_n, seq_n, rows // seq_n, width), in_weight.dtype),
        in_specs=[VM],
        out_specs=pl.BlockSpec(memory_space=pl.ANY),
        scratch_shapes=[dma(()), dma((3,)), dma((4,)), dma((3,)), dma((3,)), dma((3,)), dma((3,)),
                        dma((3, 2)), dma((3, 2)), dma((3, 5)), dma((3, 5))],
        compiler_params=pltpu.CompilerParams(collective_id=2, has_side_effects=True),
    )(in_weight.reshape(seq_n, rows // seq_n, width))
    return out.reshape(dp_n * rows, width)


def grads_kernel(dp_n, seq_n, p_ref, kp_ref, o_ref, ko_ref, r0, acc, sa, sb, ra, rb, sa2, sb2, ra2,
                 rb2, kb1, km, kb2, ws, wr, k1s, k1r, k2s, k2r, k3s, k3r):
    d, s = lax.axis_index("dp"), lax.axis_index("seq")
    c, x, y, sx, sy, sd, sc = square_at(s)
    plane = ring_peers(s, seq_n)
    line = ring_peers(d, dp_n)
    px, py, pc = at(d, sx), at(d, sy), at(d, sc)
    rows = p_ref.shape[0]
    h, q, e, t = rows // 2, rows // 4, rows // 8, rows // 16

    def span(start, size):
        return pl.ds(pl.multiple_of(start, 16), size)

    def each(size, fn):
        @pl.loop(0, size // 16)
        def _(i):
            fn(pl.multiple_of(i * 16, 16))

    greet([at(d, j) for j in plane] + [at(j, s) for j in line])
    first = remote(p_ref.at[span((1 - c) * h, h)], r0, ws.at[0], wr.at[0], pc)
    first.start()
    for k, j in enumerate(plane):
        remote(kp_ref.at[j], kb1.at[s], k1s.at[k], k1r.at[s], at(d, j)).start()
    kb1[s] = kp_ref[s]
    for k, j in enumerate(plane):
        copy = remote(kp_ref.at[j], kb1.at[j], k1s.at[k], k1r.at[j], at(d, j))
        copy.wait_recv()
        copy.wait_send()
    km[...] = merge([kb1[j] for j in range(seq_n)], False)
    for k, j in enumerate(line):
        remote(km, kb2.at[d], k2s.at[k], k2r.at[d], at(j, s)).start()
    kb2[d] = km[...]
    first.wait()

    def add0(i):
        acc[pl.ds(i, 16)] = p_ref[span(c * h + i, 16)] + r0[pl.ds(i, 16)]

    each(h, add0)

    def pack1(i):
        sa[pl.ds(i, 16)] = acc[span((1 - x) * e + i, 16)].astype(jnp.bfloat16)
        sb[pl.ds(i, 16)] = acc[span(q + (1 - y) * e + i, 16)].astype(jnp.bfloat16)

    each(e, pack1)
    one = remote(sa, ra, ws.at[1], wr.at[1], px)
    two = remote(sb, rb, ws.at[2], wr.at[2], py)
    one.start()
    two.start()
    for k, j in enumerate(line):
        copy = remote(km, kb2.at[j], k2s.at[k], k2r.at[j], at(j, s))
        copy.wait_recv()
        copy.wait_send()
    ko_ref[s] = merge([kb2[j] for j in range(dp_n)], False)
    for k, j in enumerate(plane):
        remote(ko_ref.at[s], ko_ref.at[s], k3s.at[k], k3r.at[s], at(d, j)).start()
    one.wait()
    two.wait()

    def pack2(i):
        away_a, away_b = (1 - y) * t + i, (1 - x) * t + i
        sa2[pl.ds(i, 16)] = (
            acc[span(x * e + away_a, 16)] + ra[span(away_a, 16)].astype(jnp.float32)
        ).astype(jnp.bfloat16)
        sb2[pl.ds(i, 16)] = (
            acc[span(q + y * e + away_b, 16)] + rb[span(away_b, 16)].astype(jnp.float32)
        ).astype(jnp.bfloat16)

    each(t, pack2)
    one = remote(sa2, ra2, ws.at[3], wr.at[3], py)
    two = remote(sb2, rb2, ws.at[4], wr.at[4], px)
    one.start()
    two.start()
    one.wait()
    two.wait()

    def last(i):
        keep_a, keep_b = y * t + i, x * t + i
        o_ref[span(c * h + x * e + keep_a, 16)] = (
            acc[span(x * e + keep_a, 16)] + ra[span(keep_a, 16)].astype(jnp.float32)
            + ra2[pl.ds(i, 16)].astype(jnp.float32)
        ).astype(jnp.bfloat16)
        o_ref[span(c * h + q + y * e + keep_b, 16)] = (
            acc[span(q + y * e + keep_b, 16)] + rb[span(keep_b, 16)].astype(jnp.float32)
            + rb2[pl.ds(i, 16)].astype(jnp.float32)
        ).astype(jnp.bfloat16)

    each(t, last)

    def swap(mine, other, n, peer):
        copy = remote(o_ref.at[mine], o_ref.at[mine], ws.at[n], wr.at[n], peer)
        copy.start()
        return copy, remote(o_ref.at[other], o_ref.at[other], ws.at[n], wr.at[n], peer)

    def finish(pairs):
        for copy, arrival in pairs:
            arrival.wait_recv()
        for copy, arrival in pairs:
            copy.wait_send()

    base = c * h
    finish([
        swap(span(base + x * e + y * t, t), span(base + x * e + (1 - y) * t, t), 5, py),
        swap(span(base + q + y * e + x * t, t), span(base + q + y * e + (1 - x) * t, t), 6, px),
    ])
    finish([
        swap(span(base + x * e, e), span(base + (1 - x) * e, e), 7, px),
        swap(span(base + q + y * e, e), span(base + q + (1 - y) * e, e), 8, py),
    ])
    finish([swap(span(base, h), span((1 - c) * h, h), 9, pc)])
    for k, j in enumerate(plane):
        remote(ko_ref.at[j], ko_ref.at[j], k3s.at[k], k3r.at[j], at(d, j)).wait_recv()
        remote(ko_ref.at[s], ko_ref.at[s], k3s.at[k], k3r.at[s], at(d, j)).wait_send()


def sum_grads(partial, kernel_part):
    dp_n, seq_n = lax.axis_size("dp"), lax.axis_size("seq")
    rows, width = partial.shape
    taps, channels = kernel_part.shape
    packed = jnp.pad(kernel_part, ((0, 1), (0, 0))).reshape(seq_n, -1, 128)
    block = packed.shape[1:]
    dma = pltpu.SemaphoreType.DMA
    bf = jnp.bfloat16
    summed, taps_sum = pl.pallas_call(
        functools.partial(grads_kernel, dp_n, seq_n),
        out_shape=(
            jax.ShapeDtypeStruct((rows, width), bf),
            jax.ShapeDtypeStruct(packed.shape, jnp.float32),
        ),
        in_specs=[VM, VM],
        out_specs=(VM, VM),
        scratch_shapes=[
            pltpu.VMEM((rows // 2, width), jnp.float32),
            pltpu.VMEM((rows // 2, width), jnp.float32),
            pltpu.VMEM((rows // 8, width), bf),
            pltpu.VMEM((rows // 8, width), bf),
            pltpu.VMEM((rows // 8, width), bf),
            pltpu.VMEM((rows // 8, width), bf),
            pltpu.VMEM((rows // 16, width), bf),
            pltpu.VMEM((rows // 16, width), bf),
            pltpu.VMEM((rows // 16, width), bf),
            pltpu.VMEM((rows // 16, width), bf),
            pltpu.VMEM((seq_n,) + block, jnp.float32),
            pltpu.VMEM(block, jnp.float32),
            pltpu.VMEM((dp_n,) + block, jnp.float32),
            dma((10,)), dma((10,)),
            dma((seq_n,)), dma((seq_n,)), dma((dp_n,)), dma((dp_n,)), dma((seq_n,)), dma((seq_n,)),
        ],
        compiler_params=pltpu.CompilerParams(collective_id=3, has_side_effects=True),
    )(partial, packed)
    return summed.astype(jnp.float32), taps_sum.reshape(taps + 1, channels)[:taps]


def padded_2(cells, sides, width):
    for axis, dim in sides:
        count = lax.axis_size(axis)
        ends = count - 1
        head = lax.slice_in_dim(cells, 0, width, axis=dim)
        tail = lax.slice_in_dim(cells, cells.shape[dim] - width, cells.shape[dim], axis=dim)
        cells = jnp.concatenate(
            [
                lax.ppermute(tail, axis, [(i, (i + 1) % count) for i in range(ends)]),
                cells,
                lax.ppermute(head, axis, [((i + 1) % count, i) for i in range(ends)]),
            ],
            axis=dim,
        )
    return cells


def restore(quantized, scales):
    per_channel = jnp.repeat(scales.T, 128, axis=1)
    return (quantized.astype(jnp.float32) * per_channel).astype(jnp.bfloat16)


def depthwise(padded, kernel, frames):
    running = jnp.zeros((frames, padded.shape[1]), jnp.float32)
    for offset in range(kernel.shape[0]):
        running = running + kernel[offset] * padded[offset : offset + frames].astype(jnp.float32)
    return running


def per_device(
    saved_codes, code_scales, lengths, in_weight, conv_kernel, bn_gain, bn_shift, out_grad
):
    frames = saved_codes.shape[1]
    feature_width = saved_codes.shape[2]
    tap_count = conv_kernel.shape[0]
    half_span = (tap_count - 1) // 2
    groups = lengths.shape[0]
    group_at = lax.axis_index("dp")
    length = jnp.sum(jnp.where(jnp.arange(groups, dtype=jnp.int32) == group_at, lengths, 0))
    counted = jnp.sum(lengths).astype(jnp.float32)
    first_frame = lax.axis_index("seq") * frames
    valid_mask = (first_frame + jnp.arange(frames, dtype=jnp.int32) < length).astype(jnp.float32)[
        :, None
    ]
    restored = restore(saved_codes[0], code_scales[0])
    square = lax.axis_size("dp") == 4 and lax.axis_size("seq") == 8
    if square:
        weights = gather_weights(in_weight)
    else:
        weights = lax.all_gather(in_weight, "dp", axis=0, tiled=True)
    pre_act = lax.dot_general(
        restored, weights, (((1,), (1,)), ((), ())), preferred_element_type=jnp.float32
    )
    linear = pre_act[:, :feature_width]
    gate_part = jax.nn.sigmoid(pre_act[:, feature_width:])
    gated = (linear * gate_part * valid_mask).astype(jnp.bfloat16)
    gated_pad = padded_2(gated, (("seq", 0),), half_span)
    conv_out = depthwise(gated_pad, conv_kernel, frames)
    own_sum = jnp.sum(conv_out * valid_mask, axis=0)
    own_count = jnp.sum(valid_mask)
    centered = (conv_out - own_sum / jnp.maximum(own_count, 1.0)) * valid_mask
    own_square = jnp.sum(centered * centered, axis=0)
    total, spread, _ = sum_all(
        [own_sum, own_square, jnp.full_like(own_sum, own_count)], True, 0
    )
    mean_value = total / counted
    variance = spread / counted
    inverse = lax.rsqrt(variance + EPS)
    normed = (conv_out - mean_value) * inverse
    shaped = bn_gain * normed + bn_shift
    smooth = jax.nn.sigmoid(shaped)
    grad_shaped = (
        out_grad[0].astype(jnp.float32) * valid_mask * smooth * (1.0 + shaped * (1.0 - smooth))
    )
    shift_grad, gain_grad = sum_all(
        [jnp.sum(grad_shaped, axis=0), jnp.sum(grad_shaped * normed, axis=0)], False, 1
    )
    grad_conv = (
        bn_gain * inverse * (grad_shaped - (shift_grad + normed * gain_grad) / counted) * valid_mask
    )
    kernel_part = jnp.stack(
        [
            jnp.sum(grad_conv * gated_pad[offset : offset + frames].astype(jnp.float32), axis=0)
            for offset in range(tap_count)
        ]
    )
    grad_pad = padded_2(grad_conv, (("seq", 0),), half_span)
    grad_gated = depthwise(grad_pad, conv_kernel[::-1], frames) * valid_mask
    grad_pre = jnp.concatenate(
        [grad_gated * gate_part, grad_gated * linear * gate_part * (1.0 - gate_part)], axis=1
    ).astype(jnp.bfloat16)
    in_grad = jnp.dot(grad_pre, weights, preferred_element_type=jnp.float32)
    own_columns = lax.all_to_all(grad_pre[None], "dp", split_axis=2, concat_axis=0, tiled=True)
    local_rows = lax.dot_general(
        own_columns,
        lax.all_gather(restored[None], "dp", axis=0, tiled=True),
        (((0, 1), (0, 1)), ((), ())),
        preferred_element_type=jnp.float32,
    )
    if square:
        weight_grad, kernel_grad = sum_grads(local_rows, kernel_part)
    else:
        weight_grad = lax.psum(local_rows, "seq")
        kernel_grad = lax.psum(kernel_part, ("dp", "seq"))
    return (in_grad.astype(jnp.bfloat16)[None], weight_grad, kernel_grad, gain_grad, shift_grad)


def solution(mesh):
    in_specs = (
        P("dp", "seq", None),
        P("dp", None, "seq"),
        P(),
        P("dp", None),
        P(),
        P(),
        P(),
        P("dp", "seq", None),
    )
    out_specs = (P("dp", "seq", None), P("dp", None), P(), P(), P())
    return jax.shard_map(
        per_device, mesh=mesh, in_specs=in_specs, out_specs=out_specs, check_vma=False
    )
```

```python
import functools

import jax
import jax.numpy as jnp
from jax import lax
from jax.experimental import pallas as pl
from jax.experimental.pallas import tpu as pltpu
from jax.sharding import PartitionSpec as P

EPS = 1e-05
MESH = pl.DeviceIdType.MESH
VM = pl.BlockSpec(memory_space=pltpu.VMEM)


def at(d, s):
    return {"dp": d, "seq": s}


def greet(peers):
    barrier = pltpu.get_barrier_semaphore()
    for peer in peers:
        pl.semaphore_signal(barrier, inc=1, device_id=peer, device_id_type=MESH)
    pl.semaphore_wait(barrier, len(peers))


def remote(src, dst, send, recv, peer):
    return pltpu.make_async_remote_copy(
        src_ref=src, dst_ref=dst, send_sem=send, recv_sem=recv, device_id=peer, device_id_type=MESH
    )


def ring_peers(me, count):
    return [lax.rem(me + k, count) for k in range(1, count)]


def total_of(parts):
    return functools.reduce(lambda a, b: a + b, parts)


def merge_moments(parts, counts):
    count = functools.reduce(lambda a, b: a + b, counts)
    total = total_of([part[0:1] for part in parts])
    mean = total / jnp.maximum(count, 1.0)
    spread = total_of([part[1:2] for part in parts])
    for part, n in zip(parts, counts):
        shift = part[0:1] / jnp.maximum(n, 1.0) - mean
        spread = spread + n * (shift * shift)
    return total, spread


def middle_kernel(dp_n, seq_n, pre_ref, len_ref, taps_ref, gain_ref, bias_ref, up_ref,
                  cols_ref, kp_ref, gg_ref, sg_ref, gpre,
                  gp, gcp, co, gs, hs, hr, near, far, st, mid, near2, far2, st2, mid2,
                  h_s, h_r, g_s, g_r, s1, r1, s2, r2, s3, r3, s4, r4, as_, ar_):
    d, s = lax.axis_index("dp"), lax.axis_index("seq")
    frames, width = up_ref.shape
    taps = taps_ref.shape[0]
    plane = ring_peers(s, seq_n)
    line = ring_peers(d, dp_n)
    left, right = lax.rem(s + seq_n - 1, seq_n), lax.rem(s + 1, seq_n)
    length = len_ref[d]
    lengths = [len_ref[g] for g in range(dp_n)]
    counted = functools.reduce(lambda a, b: a + b, lengths).astype(jnp.float32)

    def share(j):
        return jnp.clip(length - j * frames, 0, frames).astype(jnp.float32)

    own_count = share(s)
    row = lax.broadcasted_iota(jnp.int32, (frames, 1), 0) + s * frames
    mask = jnp.broadcast_to((row < length).astype(jnp.float32), (frames, 128))
    keep_left = jnp.where(s == 0, 0.0, 1.0).astype(jnp.float32)
    keep_right = jnp.where(s == seq_n - 1, 0.0, 1.0).astype(jnp.float32)
    body = pl.ds(16, frames)
    tail = frames + 16

    def blocks(fn):
        @pl.loop(0, width // 128)
        def _(i):
            fn(pl.ds(pl.multiple_of(i * 128, 128), 128),
               pl.ds(pl.multiple_of(width + i * 128, 128), 128))

    def gate(a, b):
        g = jax.nn.sigmoid(pre_ref[:, b])
        value = (pre_ref[:, a] * g * mask).astype(jnp.bfloat16)
        gp[body, a] = value.astype(jnp.float32)
        hs[0, :, a] = value[0:16]
        hs[1, :, a] = value[frames - 16 : frames]

    blocks(gate)
    greet([at(d, j) for j in plane] + [at(j, s) for j in line])
    to_left = remote(hs.at[0], hr.at[1], h_s.at[0], h_r.at[1], at(d, left))
    to_right = remote(hs.at[1], hr.at[0], h_s.at[1], h_r.at[0], at(d, right))
    to_left.start()
    to_right.start()
    to_left.wait()
    to_right.wait()

    def conv(a, b):
        gp[0:16, a] = hr[0, :, a].astype(jnp.float32) * keep_left
        gp[tail : tail + 16, a] = hr[1, :, a].astype(jnp.float32) * keep_right
        out = taps_ref[0:1, a] * gp[1 : 1 + frames, a]
        for k in range(1, taps):
            out = out + taps_ref[k : k + 1, a] * gp[k + 1 : k + 1 + frames, a]
        co[:, a] = out
        total = jnp.sum(out * mask, axis=0, keepdims=True)
        centered = (out - total / jnp.maximum(own_count, 1.0)) * mask
        st[0:1, a] = total
        st[1:2, a] = jnp.sum(centered * centered, axis=0, keepdims=True)

    blocks(conv)

    def exchange(mine, slots, me, peers, where, send, recv):
        for k, j in enumerate(peers):
            remote(mine, slots.at[me], send.at[k], recv.at[me], where(j)).start()
        slots[me] = mine[...]
        for k, j in enumerate(peers):
            copy = remote(mine, slots.at[j], send.at[k], recv.at[j], where(j))
            copy.wait_recv()
            copy.wait_send()

    exchange(st, near, s, plane, lambda j: at(d, j), s1, r1)
    total, spread = merge_moments([near[j] for j in range(seq_n)], [share(j) for j in range(seq_n)])
    mid[0:1] = total
    mid[1:2] = spread
    exchange(mid, far, d, line, lambda j: at(j, s), s2, r2)
    total, spread = merge_moments(
        [far[j] for j in range(dp_n)], [n.astype(jnp.float32) for n in lengths]
    )
    mid[0:1] = total / counted
    mid[1:2] = lax.rsqrt(spread / counted + EPS)

    def shape(a, b):
        normed = (co[:, a] - mid[0:1, a]) * mid[1:2, a]
        shaped = gain_ref[:, a] * normed + bias_ref[:, a]
        smooth = jax.nn.sigmoid(shaped)
        grad = up_ref[:, a].astype(jnp.float32) * mask * smooth * (1.0 + shaped * (1.0 - smooth))
        co[:, a] = normed
        gs[:, a] = grad
        st2[0:1, a] = jnp.sum(grad, axis=0, keepdims=True)
        st2[1:2, a] = jnp.sum(grad * normed, axis=0, keepdims=True)

    blocks(shape)
    exchange(st2, near2, s, plane, lambda j: at(d, j), s3, r3)
    mid2[...] = total_of([near2[j] for j in range(seq_n)])
    exchange(mid2, far2, d, line, lambda j: at(j, s), s4, r4)
    both = total_of([far2[j] for j in range(dp_n)])
    sg_ref[...] = both[0:1]
    gg_ref[...] = both[1:2]

    def back(a, b):
        scale = gain_ref[:, a] * mid[1:2, a]
        gcp[body, a] = (
            scale * (gs[:, a] - (sg_ref[:, a] + co[:, a] * gg_ref[:, a]) / counted) * mask
        )

    blocks(back)
    to_left = remote(
        gcp.at[pl.ds(16, 16)], gcp.at[pl.ds(tail, 16)], g_s.at[0], g_r.at[1], at(d, left)
    )
    to_right = remote(
        gcp.at[pl.ds(tail - 16, 16)], gcp.at[pl.ds(0, 16)], g_s.at[1], g_r.at[0], at(d, right)
    )
    to_left.start()
    to_right.start()
    to_left.wait()
    to_right.wait()
    gcp[0:16] = gcp[0:16] * keep_left
    gcp[tail : tail + 16] = gcp[tail : tail + 16] * keep_right
    part = 2 * width // dp_n

    def unconv(half):
        def fn(i, a, b, a_out, b_out):
            out = taps_ref[0:1, a] * gcp[taps : taps + frames, a]
            for k in range(1, taps):
                out = out + taps_ref[k : k + 1, a] * gcp[taps - k : taps - k + frames, a]
            out = out * mask
            g = jax.nn.sigmoid(pre_ref[:, b])
            gpre[half, :, a_out] = (out * g).astype(jnp.bfloat16)
            gpre[dp_n // 2 + half, :, a_out] = (
                out * pre_ref[:, a] * g * (1.0 - g)
            ).astype(jnp.bfloat16)

        @pl.loop(0, part // 128)
        def _(i):
            start = half * part + i * 128
            fn(i, pl.ds(pl.multiple_of(start, 128), 128),
               pl.ds(pl.multiple_of(width + start, 128), 128),
               pl.ds(pl.multiple_of(i * 128, 128), 128), None)

    for half in range(dp_n // 2):
        unconv(half)
    for k, j in enumerate(line):
        remote(gpre.at[j], cols_ref.at[d], as_.at[k], ar_.at[d], at(j, s)).start()
    cols_ref[d] = gpre[d]

    def tap_grads(a, b):
        grad = gcp[body, a]
        for k in range(taps):
            kp_ref[k : k + 1, a] = jnp.sum(
                grad * gp[k + 1 : k + 1 + frames, a], axis=0, keepdims=True
            )
        kp_ref[taps : taps + 1, a] = jnp.zeros((1, 128), jnp.float32)

    blocks(tap_grads)
    for k, j in enumerate(line):
        copy = remote(gpre.at[j], cols_ref.at[j], as_.at[k], ar_.at[j], at(j, s))
        copy.wait_recv()
        copy.wait_send()


def middle(pre_act, lengths, taps, gain, bias, up):
    dp_n, seq_n = lax.axis_size("dp"), lax.axis_size("seq")
    frames, width = up.shape
    f32, bf, dma = jnp.float32, jnp.bfloat16, pltpu.SemaphoreType.DMA
    pair = (2, width)
    block = (dp_n, frames, 2 * width // dp_n)
    return pl.pallas_call(
        functools.partial(middle_kernel, dp_n, seq_n),
        out_shape=(
            jax.ShapeDtypeStruct(block, bf),
            jax.ShapeDtypeStruct((taps.shape[0] + 1, width), f32),
            jax.ShapeDtypeStruct((1, width), f32),
            jax.ShapeDtypeStruct((1, width), f32),
            jax.ShapeDtypeStruct(block, bf),
        ),
        in_specs=[VM, pl.BlockSpec(memory_space=pltpu.SMEM), VM, VM, VM, VM],
        out_specs=(VM, VM, VM, VM, VM),
        scratch_shapes=[
            pltpu.VMEM((frames + 32, width), f32),
            pltpu.VMEM((frames + 32, width), f32),
            pltpu.VMEM((frames, width), f32),
            pltpu.VMEM((frames, width), f32),
            pltpu.VMEM((2, 16, width), bf),
            pltpu.VMEM((2, 16, width), bf),
            pltpu.VMEM((seq_n,) + pair, f32),
            pltpu.VMEM((dp_n,) + pair, f32),
            pltpu.VMEM(pair, f32),
            pltpu.VMEM(pair, f32),
            pltpu.VMEM((seq_n,) + pair, f32),
            pltpu.VMEM((dp_n,) + pair, f32),
            pltpu.VMEM(pair, f32),
            pltpu.VMEM(pair, f32),
            dma((2,)), dma((2,)), dma((2,)), dma((2,)),
            dma((seq_n,)), dma((seq_n,)), dma((dp_n,)), dma((dp_n,)),
            dma((seq_n,)), dma((seq_n,)), dma((dp_n,)), dma((dp_n,)),
            dma((dp_n,)), dma((dp_n,)),
        ],
        compiler_params=pltpu.CompilerParams(collective_id=0, has_side_effects=True),
    )(pre_act, lengths, taps, gain[None], bias[None], up)


def square_at(s):
    c, x, y = lax.rem(s, 2), lax.rem(s // 2, 2), s // 4
    sx = (y * 2 + (1 - x)) * 2 + c
    sy = ((1 - y) * 2 + x) * 2 + c
    sd = ((1 - y) * 2 + (1 - x)) * 2 + c
    sc = (y * 2 + x) * 2 + (1 - c)
    return c, x, y, sx, sy, sd, sc


def weights_kernel(w_ref, codes_ref, scale_ref, out, x_all, x_ref, local, bs, br, zs, zr, xs, xr, ys, yr, fs, fr, cs, cr):
    d, s = lax.axis_index("dp"), lax.axis_index("seq")
    c, x, y, sx, sy, sd, sc = square_at(s)
    rows = w_ref.shape[1]
    half = rows // 2
    low, high = pl.ds(0, half), pl.ds(half, half)
    line = [d + 1 - 2 * lax.rem(d, 2), 2 - d // 2, 3 - 3 * (d // 2)]
    px, py, pc = at(d, sx), at(d, sy), at(d, sc)
    greet([at(j, s) for j in line] + [px, py, pc])
    for k, j in enumerate(line):
        remote(w_ref.at[s], out.at[d, s], zs.at[k], zr.at[d], at(j, s)).start()
    own = pltpu.make_async_copy(w_ref, out.at[d], local.at[0])
    own.start()
    for i in range(scale_ref.shape[1]):
        cols = slice(i * 128, i * 128 + 128)
        x_ref[:, cols] = (
            codes_ref[:, cols].astype(jnp.float32) * scale_ref[:, i : i + 1]
        ).astype(jnp.bfloat16)
    for k, j in enumerate(line):
        remote(x_ref, x_all.at[d], bs.at[k], br.at[d], at(j, s)).start()
    keep = pltpu.make_async_copy(x_ref, x_all.at[d], local.at[1])
    keep.start()
    pending = []
    core = []

    def to_core(k, n, ref, other):
        copy = remote(ref, ref, cs.at[k, n], cr.at[k, n], pc)
        copy.start()
        pending.append(copy)
        core.append(remote(other, other, cs.at[k, n], cr.at[k, n], pc))

    cx, cy, cd = sx + 1 - 2 * c, sy + 1 - 2 * c, sd + 1 - 2 * c
    for k, j in enumerate(line):
        mine = out.at[j, s]
        remote(mine, mine, zs.at[k], zr.at[j], at(j, s)).wait_recv()
        for send, recv, peer in ((xs, xr, px), (ys, yr, py)):
            copy = remote(mine, mine, send.at[k], recv.at[k], peer)
            copy.start()
            pending.append(copy)
        to_core(k, 0, mine, out.at[j, sc])
    for k, j in enumerate(line):
        remote(out.at[j, sx], out.at[j, sx], xs.at[k], xr.at[k], px).wait_recv()
        part = out.at[j, sx, low]
        copy = remote(part, part, fs.at[k, 0], fr.at[k, 0], py)
        copy.start()
        pending.append(copy)
        to_core(k, 1, out.at[j, sx], out.at[j, cx])
        remote(out.at[j, sy], out.at[j, sy], ys.at[k], yr.at[k], py).wait_recv()
        part = out.at[j, sy, high]
        copy = remote(part, part, fs.at[k, 1], fr.at[k, 1], px)
        copy.start()
        pending.append(copy)
        to_core(k, 2, out.at[j, sy], out.at[j, cy])
    for k, j in enumerate(line):
        part = out.at[j, sd, low]
        remote(part, part, fs.at[k, 0], fr.at[k, 0], py).wait_recv()
        to_core(k, 3, part, out.at[j, cd, low])
        part = out.at[j, sd, high]
        remote(part, part, fs.at[k, 1], fr.at[k, 1], px).wait_recv()
        to_core(k, 4, part, out.at[j, cd, high])
    for copy in core:
        copy.wait_recv()
    for copy in pending:
        copy.wait_send()
    for k, j in enumerate(line):
        remote(w_ref.at[s], out.at[d, s], zs.at[k], zr.at[d], at(j, s)).wait_send()
    for k, j in enumerate(line):
        copy = remote(x_ref, x_all.at[j], bs.at[k], br.at[j], at(j, s))
        copy.wait_recv()
        copy.wait_send()
    own.wait()
    keep.wait()


def gather_weights(in_weight, codes, scales):
    dp_n, seq_n = lax.axis_size("dp"), lax.axis_size("seq")
    rows, width = in_weight.shape
    dma = pltpu.SemaphoreType.DMA
    hbm = pl.BlockSpec(memory_space=pl.ANY)
    out, x_all, x = pl.pallas_call(
        weights_kernel,
        out_shape=(
            jax.ShapeDtypeStruct((dp_n, seq_n, rows // seq_n, width), in_weight.dtype),
            jax.ShapeDtypeStruct((dp_n,) + codes.shape, codes.dtype),
            jax.ShapeDtypeStruct(codes.shape, codes.dtype),
        ),
        in_specs=[VM, VM, VM],
        out_specs=(hbm, hbm, VM),
        scratch_shapes=[dma((2,)), dma((3,)), dma((4,)), dma((3,)), dma((4,)), dma((3,)), dma((3,)), dma((3,)), dma((3,)),
                        dma((3, 2)), dma((3, 2)), dma((3, 5)), dma((3, 5))],
        compiler_params=pltpu.CompilerParams(collective_id=2, has_side_effects=True),
    )(in_weight.reshape(seq_n, rows // seq_n, width), codes, scales.T)
    return out.reshape(dp_n * rows, width), x_all, x


def grads_kernel(dp_n, seq_n, p_ref, kp_ref, o_ref, ko_ref, r0, acc, sa, sb, ra, rb, sa2, sb2, ra2,
                 rb2, kb1, km, kb2, ws, wr, k1s, k1r, k2s, k2r, k3s, k3r):
    d, s = lax.axis_index("dp"), lax.axis_index("seq")
    c, x, y, sx, sy, sd, sc = square_at(s)
    plane = ring_peers(s, seq_n)
    line = ring_peers(d, dp_n)
    px, py, pc = at(d, sx), at(d, sy), at(d, sc)
    rows = p_ref.shape[0]
    h, q, e, t = rows // 2, rows // 4, rows // 8, rows // 16

    def span(start, size):
        return pl.ds(pl.multiple_of(start, 16), size)

    def each(size, fn):
        @pl.loop(0, size // 16)
        def _(i):
            fn(pl.multiple_of(i * 16, 16))

    greet([at(d, j) for j in plane] + [at(j, s) for j in line])
    first = remote(p_ref.at[span((1 - c) * h, h)], r0, ws.at[0], wr.at[0], pc)
    first.start()
    for k, j in enumerate(plane):
        remote(kp_ref.at[j], kb1.at[s], k1s.at[k], k1r.at[s], at(d, j)).start()
    kb1[s] = kp_ref[s]
    for k, j in enumerate(plane):
        copy = remote(kp_ref.at[j], kb1.at[j], k1s.at[k], k1r.at[j], at(d, j))
        copy.wait_recv()
        copy.wait_send()
    km[...] = total_of([kb1[j] for j in range(seq_n)])
    for k, j in enumerate(line):
        remote(km, kb2.at[d], k2s.at[k], k2r.at[d], at(j, s)).start()
    kb2[d] = km[...]
    first.wait()

    def add0(i):
        acc[pl.ds(i, 16)] = p_ref[span(c * h + i, 16)] + r0[pl.ds(i, 16)]

    each(h, add0)

    def pack1(i):
        sa[pl.ds(i, 16)] = acc[span((1 - x) * e + i, 16)].astype(jnp.bfloat16)
        sb[pl.ds(i, 16)] = acc[span(q + (1 - y) * e + i, 16)].astype(jnp.bfloat16)

    each(e, pack1)
    one = remote(sa, ra, ws.at[1], wr.at[1], px)
    two = remote(sb, rb, ws.at[2], wr.at[2], py)
    one.start()
    two.start()
    for k, j in enumerate(line):
        copy = remote(km, kb2.at[j], k2s.at[k], k2r.at[j], at(j, s))
        copy.wait_recv()
        copy.wait_send()
    ko_ref[s] = total_of([kb2[j] for j in range(dp_n)])
    for k, j in enumerate(plane):
        remote(ko_ref.at[s], ko_ref.at[s], k3s.at[k], k3r.at[s], at(d, j)).start()
    one.wait()
    two.wait()

    def pack2(i):
        away_a, away_b = (1 - y) * t + i, (1 - x) * t + i
        sa2[pl.ds(i, 16)] = (
            acc[span(x * e + away_a, 16)] + ra[span(away_a, 16)].astype(jnp.float32)
        ).astype(jnp.bfloat16)
        sb2[pl.ds(i, 16)] = (
            acc[span(q + y * e + away_b, 16)] + rb[span(away_b, 16)].astype(jnp.float32)
        ).astype(jnp.bfloat16)

    each(t, pack2)
    one = remote(sa2, ra2, ws.at[3], wr.at[3], py)
    two = remote(sb2, rb2, ws.at[4], wr.at[4], px)
    one.start()
    two.start()
    one.wait()
    two.wait()

    def last(i):
        keep_a, keep_b = y * t + i, x * t + i
        o_ref[span(c * h + x * e + keep_a, 16)] = (
            acc[span(x * e + keep_a, 16)] + ra[span(keep_a, 16)].astype(jnp.float32)
            + ra2[pl.ds(i, 16)].astype(jnp.float32)
        ).astype(jnp.bfloat16)
        o_ref[span(c * h + q + y * e + keep_b, 16)] = (
            acc[span(q + y * e + keep_b, 16)] + rb[span(keep_b, 16)].astype(jnp.float32)
            + rb2[pl.ds(i, 16)].astype(jnp.float32)
        ).astype(jnp.bfloat16)

    each(t, last)

    def swap(mine, other, n, peer):
        copy = remote(o_ref.at[mine], o_ref.at[mine], ws.at[n], wr.at[n], peer)
        copy.start()
        return copy, remote(o_ref.at[other], o_ref.at[other], ws.at[n], wr.at[n], peer)

    def finish(pairs):
        for copy, arrival in pairs:
            arrival.wait_recv()
        for copy, arrival in pairs:
            copy.wait_send()

    base = c * h
    finish([
        swap(span(base + x * e + y * t, t), span(base + x * e + (1 - y) * t, t), 5, py),
        swap(span(base + q + y * e + x * t, t), span(base + q + y * e + (1 - x) * t, t), 6, px),
    ])
    finish([
        swap(span(base + x * e, e), span(base + (1 - x) * e, e), 7, px),
        swap(span(base + q + y * e, e), span(base + q + (1 - y) * e, e), 8, py),
    ])
    finish([swap(span(base, h), span((1 - c) * h, h), 9, pc)])
    for k, j in enumerate(plane):
        remote(ko_ref.at[j], ko_ref.at[j], k3s.at[k], k3r.at[j], at(d, j)).wait_recv()
        remote(ko_ref.at[s], ko_ref.at[s], k3s.at[k], k3r.at[s], at(d, j)).wait_send()


def sum_grads(partial, kernel_part):
    dp_n, seq_n = lax.axis_size("dp"), lax.axis_size("seq")
    rows, width = partial.shape
    taps, channels = kernel_part.shape
    packed = kernel_part.reshape(seq_n, -1, 128)
    block = packed.shape[1:]
    dma = pltpu.SemaphoreType.DMA
    bf = jnp.bfloat16
    summed, taps_sum = pl.pallas_call(
        functools.partial(grads_kernel, dp_n, seq_n),
        out_shape=(
            jax.ShapeDtypeStruct((rows, width), bf),
            jax.ShapeDtypeStruct(packed.shape, jnp.float32),
        ),
        in_specs=[VM, VM],
        out_specs=(VM, VM),
        scratch_shapes=[
            pltpu.VMEM((rows // 2, width), jnp.float32),
            pltpu.VMEM((rows // 2, width), jnp.float32),
            pltpu.VMEM((rows // 8, width), bf),
            pltpu.VMEM((rows // 8, width), bf),
            pltpu.VMEM((rows // 8, width), bf),
            pltpu.VMEM((rows // 8, width), bf),
            pltpu.VMEM((rows // 16, width), bf),
            pltpu.VMEM((rows // 16, width), bf),
            pltpu.VMEM((rows // 16, width), bf),
            pltpu.VMEM((rows // 16, width), bf),
            pltpu.VMEM((seq_n,) + block, jnp.float32),
            pltpu.VMEM(block, jnp.float32),
            pltpu.VMEM((dp_n,) + block, jnp.float32),
            dma((10,)), dma((10,)),
            dma((seq_n,)), dma((seq_n,)), dma((dp_n,)), dma((dp_n,)), dma((seq_n,)), dma((seq_n,)),
        ],
        compiler_params=pltpu.CompilerParams(collective_id=3, has_side_effects=True),
    )(partial, packed)
    return summed.astype(jnp.float32), taps_sum.reshape(taps, channels)[: taps - 1]


def padded_2(cells, sides, width):
    for axis, dim in sides:
        count = lax.axis_size(axis)
        ends = count - 1
        head = lax.slice_in_dim(cells, 0, width, axis=dim)
        tail = lax.slice_in_dim(cells, cells.shape[dim] - width, cells.shape[dim], axis=dim)
        cells = jnp.concatenate(
            [
                lax.ppermute(tail, axis, [(i, (i + 1) % count) for i in range(ends)]),
                cells,
                lax.ppermute(head, axis, [((i + 1) % count, i) for i in range(ends)]),
            ],
            axis=dim,
        )
    return cells


def restore(quantized, scales):
    per_channel = jnp.repeat(scales.T, 128, axis=1)
    return (quantized.astype(jnp.float32) * per_channel).astype(jnp.bfloat16)


def depthwise(padded, kernel, frames):
    running = jnp.zeros((frames, padded.shape[1]), jnp.float32)
    for offset in range(kernel.shape[0]):
        running = running + kernel[offset] * padded[offset : offset + frames].astype(jnp.float32)
    return running


def plain(
    saved_codes, code_scales, lengths, in_weight, conv_kernel, bn_gain, bn_shift, out_grad
):
    frames = saved_codes.shape[1]
    feature_width = saved_codes.shape[2]
    tap_count = conv_kernel.shape[0]
    half_span = (tap_count - 1) // 2
    groups = lengths.shape[0]
    group_at = lax.axis_index("dp")
    length = jnp.sum(jnp.where(jnp.arange(groups, dtype=jnp.int32) == group_at, lengths, 0))
    counted = jnp.sum(lengths).astype(jnp.float32)
    first_frame = lax.axis_index("seq") * frames
    valid_mask = (first_frame + jnp.arange(frames, dtype=jnp.int32) < length).astype(jnp.float32)[
        :, None
    ]
    restored = restore(saved_codes[0], code_scales[0])
    weights = lax.all_gather(in_weight, "dp", axis=0, tiled=True)
    pre_act = lax.dot_general(
        restored, weights, (((1,), (1,)), ((), ())), preferred_element_type=jnp.float32
    )
    linear = pre_act[:, :feature_width]
    gate_part = jax.nn.sigmoid(pre_act[:, feature_width:])
    gated = (linear * gate_part * valid_mask).astype(jnp.bfloat16)
    gated_pad = padded_2(gated, (("seq", 0),), half_span)
    conv_out = depthwise(gated_pad, conv_kernel, frames)
    mean_value = lax.psum(jnp.sum(conv_out * valid_mask, axis=0), ("dp", "seq")) / counted
    centered = (conv_out - mean_value) * valid_mask
    variance = lax.psum(jnp.sum(centered * centered, axis=0), ("dp", "seq")) / counted
    inverse = lax.rsqrt(variance + EPS)
    normed = (conv_out - mean_value) * inverse
    shaped = bn_gain * normed + bn_shift
    smooth = jax.nn.sigmoid(shaped)
    grad_shaped = (
        out_grad[0].astype(jnp.float32) * valid_mask * smooth * (1.0 + shaped * (1.0 - smooth))
    )
    shift_grad, gain_grad = lax.psum(
        (jnp.sum(grad_shaped, axis=0), jnp.sum(grad_shaped * normed, axis=0)), ("dp", "seq")
    )
    grad_conv = (
        bn_gain * inverse * (grad_shaped - (shift_grad + normed * gain_grad) / counted) * valid_mask
    )
    kernel_part = jnp.stack(
        [
            jnp.sum(grad_conv * gated_pad[offset : offset + frames].astype(jnp.float32), axis=0)
            for offset in range(tap_count)
        ]
    )
    kernel_grad = lax.psum(kernel_part, ("dp", "seq"))
    grad_pad = padded_2(grad_conv, (("seq", 0),), half_span)
    grad_gated = depthwise(grad_pad, conv_kernel[::-1], frames) * valid_mask
    grad_pre = jnp.concatenate(
        [grad_gated * gate_part, grad_gated * linear * gate_part * (1.0 - gate_part)], axis=1
    ).astype(jnp.bfloat16)
    in_grad = jnp.dot(grad_pre, weights, preferred_element_type=jnp.float32)
    own_columns = lax.all_to_all(grad_pre[None], "dp", split_axis=2, concat_axis=0, tiled=True)
    local_rows = lax.dot_general(
        own_columns,
        lax.all_gather(restored[None], "dp", axis=0, tiled=True),
        (((0, 1), (0, 1)), ((), ())),
        preferred_element_type=jnp.float32,
    )
    weight_grad = lax.psum(local_rows, "seq")
    return (in_grad.astype(jnp.bfloat16)[None], weight_grad, kernel_grad, gain_grad, shift_grad)


def per_device(
    saved_codes, code_scales, lengths, in_weight, conv_kernel, bn_gain, bn_shift, out_grad
):
    if lax.axis_size("dp") != 4 or lax.axis_size("seq") != 8:
        return plain(
            saved_codes, code_scales, lengths, in_weight, conv_kernel, bn_gain, bn_shift, out_grad
        )
    weights, x_all, x = gather_weights(in_weight, saved_codes[0], code_scales[0])
    pre_act = lax.dot_general(
        x, weights, (((1,), (1,)), ((), ())), preferred_element_type=jnp.float32
    )
    own_columns, kernel_part, gain_grad, shift_grad, grad_pre = middle(
        pre_act, lengths, conv_kernel, bn_gain, bn_shift, out_grad[0]
    )
    local_rows = lax.dot_general(
        own_columns, x_all, (((0, 1), (0, 1)), ((), ())), preferred_element_type=jnp.float32
    )
    weight_grad, kernel_grad = sum_grads(local_rows, kernel_part)
    part = weights.shape[0] // grad_pre.shape[0]
    in_grad = lax.dot_general(
        grad_pre, weights.reshape(-1, part, weights.shape[1]), (((0, 2), (0, 1)), ((), ())),
        preferred_element_type=jnp.float32,
    )
    return (
        in_grad.astype(jnp.bfloat16)[None], weight_grad, kernel_grad, gain_grad[0], shift_grad[0]
    )


def solution(mesh):
    in_specs = (
        P("dp", "seq", None),
        P("dp", None, "seq"),
        P(),
        P("dp", None),
        P(),
        P(),
        P(),
        P("dp", "seq", None),
    )
    out_specs = (P("dp", "seq", None), P("dp", None), P(), P(), P())
    return jax.shard_map(
        per_device, mesh=mesh, in_specs=in_specs, out_specs=out_specs, check_vma=False
    )
```

```python
import functools

import jax
import jax.numpy as jnp
from jax import lax
from jax.experimental import pallas as pl
from jax.experimental.pallas import tpu as pltpu
from jax.sharding import PartitionSpec as P

EPS = 1e-05
MESH = pl.DeviceIdType.MESH
VM = pl.BlockSpec(memory_space=pltpu.VMEM)


def at(d, s):
    return {"dp": d, "seq": s}


def greet(peers):
    barrier = pltpu.get_barrier_semaphore()
    for peer in peers:
        pl.semaphore_signal(barrier, inc=1, device_id=peer, device_id_type=MESH)
    pl.semaphore_wait(barrier, len(peers))


def remote(src, dst, send, recv, peer):
    return pltpu.make_async_remote_copy(
        src_ref=src, dst_ref=dst, send_sem=send, recv_sem=recv, device_id=peer, device_id_type=MESH
    )


def ring_peers(me, count):
    return [lax.rem(me + k, count) for k in range(1, count)]


def total_of(parts):
    return functools.reduce(lambda a, b: a + b, parts)


def merge_moments(parts, counts):
    count = functools.reduce(lambda a, b: a + b, counts)
    total = total_of([part[0:1] for part in parts])
    mean = total / jnp.maximum(count, 1.0)
    spread = total_of([part[1:2] for part in parts])
    for part, n in zip(parts, counts):
        shift = part[0:1] / jnp.maximum(n, 1.0) - mean
        spread = spread + n * (shift * shift)
    return total, spread


def middle_kernel(dp_n, seq_n, pre_ref, len_ref, taps_ref, norm_ref, up_ref,
                  cols_ref, kp_ref, gg_ref, sg_ref, gpre,
                  gp, gcp, co, gs, hs, hr, near, far, st, mid, near2, far2, st2, mid2,
                  h_s, h_r, g_s, g_r, s1, r1, s2, r2, s3, r3, s4, r4, as_, ar_):
    d, s = lax.axis_index("dp"), lax.axis_index("seq")
    frames, width = up_ref.shape
    taps = taps_ref.shape[0]
    plane = ring_peers(s, seq_n)
    line = ring_peers(d, dp_n)
    left, right = lax.rem(s + seq_n - 1, seq_n), lax.rem(s + 1, seq_n)
    length = len_ref[d]
    lengths = [len_ref[g] for g in range(dp_n)]
    counted = functools.reduce(lambda a, b: a + b, lengths).astype(jnp.float32)

    def share(j):
        return jnp.clip(length - j * frames, 0, frames).astype(jnp.float32)

    own_count = share(s)
    row = lax.broadcasted_iota(jnp.int32, (frames, 1), 0) + s * frames
    mask = jnp.broadcast_to((row < length).astype(jnp.float32), (frames, 128))
    keep_left = jnp.where(s == 0, 0.0, 1.0).astype(jnp.float32)
    keep_right = jnp.where(s == seq_n - 1, 0.0, 1.0).astype(jnp.float32)
    body = pl.ds(16, frames)
    tail = frames + 16

    def blocks(fn):
        @pl.loop(0, width // 128)
        def _(i):
            fn(pl.ds(pl.multiple_of(i * 128, 128), 128),
               pl.ds(pl.multiple_of(width + i * 128, 128), 128))

    def gate(a, b):
        g = jax.nn.sigmoid(pre_ref[:, b])
        value = (pre_ref[:, a] * g * mask).astype(jnp.bfloat16)
        gp[body, a] = value.astype(jnp.float32)
        hs[0, :, a] = value[0:16]
        hs[1, :, a] = value[frames - 16 : frames]

    blocks(gate)
    greet([at(d, j) for j in plane] + [at(j, s) for j in line])
    to_left = remote(hs.at[0], hr.at[1], h_s.at[0], h_r.at[1], at(d, left))
    to_right = remote(hs.at[1], hr.at[0], h_s.at[1], h_r.at[0], at(d, right))
    to_left.start()
    to_right.start()
    to_left.wait()
    to_right.wait()

    def conv(a, b):
        gp[0:16, a] = hr[0, :, a].astype(jnp.float32) * keep_left
        gp[tail : tail + 16, a] = hr[1, :, a].astype(jnp.float32) * keep_right
        out = taps_ref[0:1, a] * gp[1 : 1 + frames, a]
        for k in range(1, taps):
            out = out + taps_ref[k : k + 1, a] * gp[k + 1 : k + 1 + frames, a]
        co[:, a] = out
        total = jnp.sum(out * mask, axis=0, keepdims=True)
        centered = (out - total / jnp.maximum(own_count, 1.0)) * mask
        st[0:1, a] = total
        st[1:2, a] = jnp.sum(centered * centered, axis=0, keepdims=True)

    blocks(conv)

    def exchange(mine, slots, me, peers, where, send, recv):
        for k, j in enumerate(peers):
            remote(mine, slots.at[me], send.at[k], recv.at[me], where(j)).start()
        slots[me] = mine[...]
        for k, j in enumerate(peers):
            copy = remote(mine, slots.at[j], send.at[k], recv.at[j], where(j))
            copy.wait_recv()
            copy.wait_send()

    exchange(st, near, s, plane, lambda j: at(d, j), s1, r1)
    total, spread = merge_moments([near[j] for j in range(seq_n)], [share(j) for j in range(seq_n)])
    mid[0:1] = total
    mid[1:2] = spread
    exchange(mid, far, d, line, lambda j: at(j, s), s2, r2)
    total, spread = merge_moments(
        [far[j] for j in range(dp_n)], [n.astype(jnp.float32) for n in lengths]
    )
    mid[0:1] = total / counted
    mid[1:2] = lax.rsqrt(spread / counted + EPS)

    def shape(a, b):
        normed = (co[:, a] - mid[0:1, a]) * mid[1:2, a]
        shaped = norm_ref[0:1, a] * normed + norm_ref[1:2, a]
        smooth = jax.nn.sigmoid(shaped)
        grad = up_ref[:, a].astype(jnp.float32) * mask * smooth * (1.0 + shaped * (1.0 - smooth))
        co[:, a] = normed
        gs[:, a] = grad
        st2[0:1, a] = jnp.sum(grad, axis=0, keepdims=True)
        st2[1:2, a] = jnp.sum(grad * normed, axis=0, keepdims=True)

    blocks(shape)
    exchange(st2, near2, s, plane, lambda j: at(d, j), s3, r3)
    mid2[...] = total_of([near2[j] for j in range(seq_n)])
    exchange(mid2, far2, d, line, lambda j: at(j, s), s4, r4)
    both = total_of([far2[j] for j in range(dp_n)])
    sg_ref[...] = both[0:1]
    gg_ref[...] = both[1:2]

    def back(a, b):
        scale = norm_ref[0:1, a] * mid[1:2, a]
        gcp[body, a] = (
            scale * (gs[:, a] - (sg_ref[:, a] + co[:, a] * gg_ref[:, a]) / counted) * mask
        )

    blocks(back)
    to_left = remote(
        gcp.at[pl.ds(16, 16)], gcp.at[pl.ds(tail, 16)], g_s.at[0], g_r.at[1], at(d, left)
    )
    to_right = remote(
        gcp.at[pl.ds(tail - 16, 16)], gcp.at[pl.ds(0, 16)], g_s.at[1], g_r.at[0], at(d, right)
    )
    to_left.start()
    to_right.start()
    to_left.wait()
    to_right.wait()
    gcp[0:16] = gcp[0:16] * keep_left
    gcp[tail : tail + 16] = gcp[tail : tail + 16] * keep_right
    part = 2 * width // dp_n

    def unconv(half):
        def fn(i, a, b, a_out, b_out):
            out = taps_ref[0:1, a] * gcp[taps : taps + frames, a]
            for k in range(1, taps):
                out = out + taps_ref[k : k + 1, a] * gcp[taps - k : taps - k + frames, a]
            out = out * mask
            g = jax.nn.sigmoid(pre_ref[:, b])
            gpre[half, :, a_out] = (out * g).astype(jnp.bfloat16)
            gpre[dp_n // 2 + half, :, a_out] = (
                out * pre_ref[:, a] * g * (1.0 - g)
            ).astype(jnp.bfloat16)

        @pl.loop(0, part // 128)
        def _(i):
            start = half * part + i * 128
            fn(i, pl.ds(pl.multiple_of(start, 128), 128),
               pl.ds(pl.multiple_of(width + start, 128), 128),
               pl.ds(pl.multiple_of(i * 128, 128), 128), None)

    for half in range(dp_n // 2):
        unconv(half)
    for k, j in enumerate(line):
        remote(gpre.at[j], cols_ref.at[d], as_.at[k], ar_.at[d], at(j, s)).start()
    cols_ref[d] = gpre[d]

    def tap_grads(a, b):
        grad = gcp[body, a]
        for k in range(taps):
            kp_ref[k : k + 1, a] = jnp.sum(
                grad * gp[k + 1 : k + 1 + frames, a], axis=0, keepdims=True
            )
        kp_ref[taps : taps + 1, a] = jnp.zeros((1, 128), jnp.float32)

    blocks(tap_grads)
    for k, j in enumerate(line):
        copy = remote(gpre.at[j], cols_ref.at[j], as_.at[k], ar_.at[j], at(j, s))
        copy.wait_recv()
        copy.wait_send()


def middle(pre_act, lengths, taps, gain, bias, up):
    dp_n, seq_n = lax.axis_size("dp"), lax.axis_size("seq")
    frames, width = up.shape
    f32, bf, dma = jnp.float32, jnp.bfloat16, pltpu.SemaphoreType.DMA
    pair = (2, width)
    block = (dp_n, frames, 2 * width // dp_n)
    return pl.pallas_call(
        functools.partial(middle_kernel, dp_n, seq_n),
        out_shape=(
            jax.ShapeDtypeStruct(block, bf),
            jax.ShapeDtypeStruct((taps.shape[0] + 1, width), f32),
            jax.ShapeDtypeStruct((1, width), f32),
            jax.ShapeDtypeStruct((1, width), f32),
            jax.ShapeDtypeStruct(block, bf),
        ),
        in_specs=[VM, pl.BlockSpec(memory_space=pltpu.SMEM), VM, VM, VM],
        out_specs=(VM, VM, VM, VM, VM),
        scratch_shapes=[
            pltpu.VMEM((frames + 32, width), f32),
            pltpu.VMEM((frames + 32, width), f32),
            pltpu.VMEM((frames, width), f32),
            pltpu.VMEM((frames, width), f32),
            pltpu.VMEM((2, 16, width), bf),
            pltpu.VMEM((2, 16, width), bf),
            pltpu.VMEM((seq_n,) + pair, f32),
            pltpu.VMEM((dp_n,) + pair, f32),
            pltpu.VMEM(pair, f32),
            pltpu.VMEM(pair, f32),
            pltpu.VMEM((seq_n,) + pair, f32),
            pltpu.VMEM((dp_n,) + pair, f32),
            pltpu.VMEM(pair, f32),
            pltpu.VMEM(pair, f32),
            dma((2,)), dma((2,)), dma((2,)), dma((2,)),
            dma((seq_n,)), dma((seq_n,)), dma((dp_n,)), dma((dp_n,)),
            dma((seq_n,)), dma((seq_n,)), dma((dp_n,)), dma((dp_n,)),
            dma((dp_n,)), dma((dp_n,)),
        ],
        compiler_params=pltpu.CompilerParams(collective_id=0, has_side_effects=True),
    )(pre_act, lengths, taps, jnp.stack([gain, bias]), up)


def square_at(s):
    c, x, y = lax.rem(s, 2), lax.rem(s // 2, 2), s // 4
    sx = (y * 2 + (1 - x)) * 2 + c
    sy = ((1 - y) * 2 + x) * 2 + c
    sd = ((1 - y) * 2 + (1 - x)) * 2 + c
    sc = (y * 2 + x) * 2 + (1 - c)
    return c, x, y, sx, sy, sd, sc


def weights_kernel(w_ref, codes_ref, scale_ref, out, x_all, x_ref, local, bu, bd, br, zu, zd, zr,
                   xs, xr, ys, yr, fs, fr, cs, cr):
    d, s = lax.axis_index("dp"), lax.axis_index("seq")
    top = br.shape[0] - 1
    c, x, y, sx, sy, sd, sc = square_at(s)
    half = w_ref.shape[1] // 2
    low, high = pl.ds(0, half), pl.ds(half, half)
    line = [d + 1 - 2 * lax.rem(d, 2), 2 - d // 2, 3 - 3 * (d // 2)]
    px, py, pc = at(d, sx), at(d, sy), at(d, sc)
    greet([at(j, s) for j in line] + [px, py, pc])

    def ends(src, dst, up, down, recv, act):
        @pl.when(d < top)
        def _():
            act(remote(src, dst, up.at[d], recv.at[d], at(d + 1, s)))

        @pl.when(d > 0)
        def _():
            act(remote(src, dst, down.at[d], recv.at[d], at(d - 1, s)))

    def hop(h, ref, up, down, recv, arrive, act):
        @pl.when(d - 1 - h >= 0)
        def _():
            j = d - 1 - h
            if arrive is not None:
                remote(ref(j), ref(j), up.at[j], recv.at[j], px).wait_recv()

            @pl.when(d < top)
            def _():
                act(remote(ref(j), ref(j), up.at[j], recv.at[j], at(d + 1, s)))

            if arrive is not None:
                arrive(j)

        @pl.when(d + 1 + h <= top)
        def _():
            j = d + 1 + h
            if arrive is not None:
                remote(ref(j), ref(j), down.at[j], recv.at[j], px).wait_recv()

            @pl.when(d > 0)
            def _():
                act(remote(ref(j), ref(j), down.at[j], recv.at[j], at(d - 1, s)))

            if arrive is not None:
                arrive(j)

    def start(copy):
        copy.start()

    def sent(copy):
        copy.wait_send()

    def nothing(j):
        pass

    def piece(j):
        return out.at[j, s]

    def frames_of(j):
        return x_all.at[j]

    ends(w_ref.at[s], out.at[d, s], zu, zd, zr, start)
    own = pltpu.make_async_copy(w_ref, out.at[d], local.at[0])
    own.start()
    for i in range(scale_ref.shape[1]):
        cols = slice(i * 128, i * 128 + 128)
        x_ref[:, cols] = (
            codes_ref[:, cols].astype(jnp.float32) * scale_ref[:, i : i + 1]
        ).astype(jnp.bfloat16)
    keep = pltpu.make_async_copy(x_ref, x_all.at[d], local.at[1])
    keep.start()
    cx, cy, cd = sx + 1 - 2 * c, sy + 1 - 2 * c, sd + 1 - 2 * c

    def spread(j):
        mine = out.at[j, s]
        return [
            remote(mine, mine, xs.at[j], xr.at[j], px),
            remote(mine, mine, ys.at[j], yr.at[j], py),
            remote(mine, mine, cs.at[j, 0], cr.at[j, 0], pc),
        ]

    def arrive(j):
        for copy in spread(j):
            copy.start()

    def own_copy(ref, send, recv, peer):
        return remote(ref, ref, send, recv, peer)

    for h in range(top):
        hop(h, piece, zu, zd, zr, arrive, start)
    ends(x_ref, x_all.at[d], bu, bd, br, start)
    pending = []

    def go(copy):
        copy.start()
        pending.append(copy)

    for k, j in enumerate(line):
        own_copy(out.at[j, sx], xs.at[j], xr.at[j], px).wait_recv()
        go(own_copy(out.at[j, sx, low], fs.at[j, 0], fr.at[j, 0], py))
        go(own_copy(out.at[j, sx], cs.at[j, 1], cr.at[j, 1], pc))
        own_copy(out.at[j, sy], ys.at[j], yr.at[j], py).wait_recv()
        go(own_copy(out.at[j, sy, high], fs.at[j, 1], fr.at[j, 1], px))
        go(own_copy(out.at[j, sy], cs.at[j, 2], cr.at[j, 2], pc))
        hop(k, frames_of, bu, bd, br, nothing, start)
    for j in line:
        part = out.at[j, sd, low]
        own_copy(part, fs.at[j, 0], fr.at[j, 0], py).wait_recv()
        go(own_copy(part, cs.at[j, 3], cr.at[j, 3], pc))
        part = out.at[j, sd, high]
        own_copy(part, fs.at[j, 1], fr.at[j, 1], px).wait_recv()
        go(own_copy(part, cs.at[j, 4], cr.at[j, 4], pc))
    for j in line:
        for n, part in enumerate((out.at[j, sc], out.at[j, cx], out.at[j, cy],
                                  out.at[j, cd, low], out.at[j, cd, high])):
            own_copy(part, cs.at[j, n], cr.at[j, n], pc).wait_recv()
        for copy in spread(j):
            copy.wait_send()
    for copy in pending:
        copy.wait_send()
    ends(w_ref.at[s], out.at[d, s], zu, zd, zr, sent)
    ends(x_ref, x_all.at[d], bu, bd, br, sent)
    for h in range(top):
        hop(h, piece, zu, zd, zr, None, sent)
        hop(h, frames_of, bu, bd, br, None, sent)
    own.wait()
    keep.wait()


def gather_weights(in_weight, codes, scales):
    dp_n, seq_n = lax.axis_size("dp"), lax.axis_size("seq")
    rows, width = in_weight.shape
    dma = pltpu.SemaphoreType.DMA
    hbm = pl.BlockSpec(memory_space=pl.ANY)
    out, x_all, x = pl.pallas_call(
        weights_kernel,
        out_shape=(
            jax.ShapeDtypeStruct((dp_n, seq_n, rows // seq_n, width), in_weight.dtype),
            jax.ShapeDtypeStruct((dp_n,) + codes.shape, codes.dtype),
            jax.ShapeDtypeStruct(codes.shape, codes.dtype),
        ),
        in_specs=[VM, VM, VM],
        out_specs=(hbm, hbm, VM),
        scratch_shapes=[dma((2,))] + [dma((dp_n,))] * 10
        + [dma((dp_n, 2)), dma((dp_n, 2)), dma((dp_n, 5)), dma((dp_n, 5))],
        compiler_params=pltpu.CompilerParams(collective_id=2, has_side_effects=True),
    )(in_weight.reshape(seq_n, rows // seq_n, width), codes, scales.T)
    return out.reshape(dp_n * rows, width), x_all, x


def grads_kernel(dp_n, seq_n, p_ref, kp_ref, g_ref, w_hbm, o_ref, ko_ref, ig_ref, wv, ia, wl, r0, acc, sa, sb, ra, rb, sa2, sb2, ra2,
                 rb2, kb1, km, kb2, ws, wr, k1s, k1r, k2s, k2r, k3s, k3r):
    d, s = lax.axis_index("dp"), lax.axis_index("seq")
    c, x, y, sx, sy, sd, sc = square_at(s)
    plane = ring_peers(s, seq_n)
    line = ring_peers(d, dp_n)
    px, py, pc = at(d, sx), at(d, sy), at(d, sc)
    rows = p_ref.shape[0]
    h, q, e, t = rows // 2, rows // 4, rows // 8, rows // 16

    def span(start, size):
        return pl.ds(pl.multiple_of(start, 16), size)

    def each(size, fn):
        @pl.loop(0, size // 16)
        def _(i):
            fn(pl.multiple_of(i * 16, 16))

    load = pltpu.make_async_copy(w_hbm, wv, wl)
    load.start()
    greet([at(d, j) for j in plane] + [at(j, s) for j in line])
    first = remote(p_ref.at[span((1 - c) * h, h)], r0, ws.at[0], wr.at[0], pc)
    first.start()
    for k, j in enumerate(plane):
        remote(kp_ref.at[j], kb1.at[s], k1s.at[k], k1r.at[s], at(d, j)).start()
    kb1[s] = kp_ref[s]
    load.wait()

    def product(j):
        return jnp.dot(g_ref[j], wv[j], preferred_element_type=jnp.float32)

    ia[...] = product(0)
    for j in range(1, dp_n // 2):
        ia[...] += product(j)
    for k, j in enumerate(plane):
        copy = remote(kp_ref.at[j], kb1.at[j], k1s.at[k], k1r.at[j], at(d, j))
        copy.wait_recv()
        copy.wait_send()
    km[...] = total_of([kb1[j] for j in range(seq_n)])
    for k, j in enumerate(line):
        remote(km, kb2.at[d], k2s.at[k], k2r.at[d], at(j, s)).start()
    kb2[d] = km[...]
    first.wait()

    def add0(i):
        acc[pl.ds(i, 16)] = p_ref[span(c * h + i, 16)] + r0[pl.ds(i, 16)]

    each(h, add0)

    def pack1(i):
        sa[pl.ds(i, 16)] = acc[span((1 - x) * e + i, 16)].astype(jnp.bfloat16)
        sb[pl.ds(i, 16)] = acc[span(q + (1 - y) * e + i, 16)].astype(jnp.bfloat16)

    each(e, pack1)
    one = remote(sa, ra, ws.at[1], wr.at[1], px)
    two = remote(sb, rb, ws.at[2], wr.at[2], py)
    one.start()
    two.start()
    for j in range(dp_n // 2, dp_n):
        ia[...] += product(j)
    ig_ref[...] = ia[...].astype(jnp.bfloat16)
    for k, j in enumerate(line):
        copy = remote(km, kb2.at[j], k2s.at[k], k2r.at[j], at(j, s))
        copy.wait_recv()
        copy.wait_send()
    ko_ref[s] = total_of([kb2[j] for j in range(dp_n)])
    for k, j in enumerate(plane):
        remote(ko_ref.at[s], ko_ref.at[s], k3s.at[k], k3r.at[s], at(d, j)).start()
    one.wait()
    two.wait()

    def pack2(i):
        away_a, away_b = (1 - y) * t + i, (1 - x) * t + i
        sa2[pl.ds(i, 16)] = (
            acc[span(x * e + away_a, 16)] + ra[span(away_a, 16)].astype(jnp.float32)
        ).astype(jnp.bfloat16)
        sb2[pl.ds(i, 16)] = (
            acc[span(q + y * e + away_b, 16)] + rb[span(away_b, 16)].astype(jnp.float32)
        ).astype(jnp.bfloat16)

    each(t, pack2)
    one = remote(sa2, ra2, ws.at[3], wr.at[3], py)
    two = remote(sb2, rb2, ws.at[4], wr.at[4], px)
    one.start()
    two.start()
    one.wait()
    two.wait()

    def last(i):
        keep_a, keep_b = y * t + i, x * t + i
        o_ref[span(c * h + x * e + keep_a, 16)] = (
            acc[span(x * e + keep_a, 16)] + ra[span(keep_a, 16)].astype(jnp.float32)
            + ra2[pl.ds(i, 16)].astype(jnp.float32)
        ).astype(jnp.bfloat16)
        o_ref[span(c * h + q + y * e + keep_b, 16)] = (
            acc[span(q + y * e + keep_b, 16)] + rb[span(keep_b, 16)].astype(jnp.float32)
            + rb2[pl.ds(i, 16)].astype(jnp.float32)
        ).astype(jnp.bfloat16)

    each(t, last)

    def swap(mine, other, n, peer):
        copy = remote(o_ref.at[mine], o_ref.at[mine], ws.at[n], wr.at[n], peer)
        copy.start()
        return copy, remote(o_ref.at[other], o_ref.at[other], ws.at[n], wr.at[n], peer)

    def finish(pairs):
        for copy, arrival in pairs:
            arrival.wait_recv()
        for copy, arrival in pairs:
            copy.wait_send()

    base = c * h
    finish([
        swap(span(base + x * e + y * t, t), span(base + x * e + (1 - y) * t, t), 5, py),
        swap(span(base + q + y * e + x * t, t), span(base + q + y * e + (1 - x) * t, t), 6, px),
    ])
    finish([
        swap(span(base + x * e, e), span(base + (1 - x) * e, e), 7, px),
        swap(span(base + q + y * e, e), span(base + q + (1 - y) * e, e), 8, py),
    ])
    finish([swap(span(base, h), span((1 - c) * h, h), 9, pc)])
    for k, j in enumerate(plane):
        remote(ko_ref.at[j], ko_ref.at[j], k3s.at[k], k3r.at[j], at(d, j)).wait_recv()
        remote(ko_ref.at[s], ko_ref.at[s], k3s.at[k], k3r.at[s], at(d, j)).wait_send()


def sum_grads(partial, kernel_part, grad_pre, weights):
    dp_n, seq_n = lax.axis_size("dp"), lax.axis_size("seq")
    rows, width = partial.shape
    taps, channels = kernel_part.shape
    packed = kernel_part.reshape(seq_n, -1, 128)
    block = packed.shape[1:]
    dma = pltpu.SemaphoreType.DMA
    bf = jnp.bfloat16
    summed, taps_sum, in_grad = pl.pallas_call(
        functools.partial(grads_kernel, dp_n, seq_n),
        out_shape=(
            jax.ShapeDtypeStruct((rows, width), bf),
            jax.ShapeDtypeStruct(packed.shape, jnp.float32),
            jax.ShapeDtypeStruct((grad_pre.shape[1], width), bf),
        ),
        in_specs=[VM, VM, VM, pl.BlockSpec(memory_space=pl.ANY)],
        out_specs=(VM, VM, VM),
        scratch_shapes=[
            pltpu.VMEM(weights.shape, bf),
            pltpu.VMEM((grad_pre.shape[1], width), jnp.float32),
            dma(()),
            pltpu.VMEM((rows // 2, width), jnp.float32),
            pltpu.VMEM((rows // 2, width), jnp.float32),
            pltpu.VMEM((rows // 8, width), bf),
            pltpu.VMEM((rows // 8, width), bf),
            pltpu.VMEM((rows // 8, width), bf),
            pltpu.VMEM((rows // 8, width), bf),
            pltpu.VMEM((rows // 16, width), bf),
            pltpu.VMEM((rows // 16, width), bf),
            pltpu.VMEM((rows // 16, width), bf),
            pltpu.VMEM((rows // 16, width), bf),
            pltpu.VMEM((seq_n,) + block, jnp.float32),
            pltpu.VMEM(block, jnp.float32),
            pltpu.VMEM((dp_n,) + block, jnp.float32),
            dma((10,)), dma((10,)),
            dma((seq_n,)), dma((seq_n,)), dma((dp_n,)), dma((dp_n,)), dma((seq_n,)), dma((seq_n,)),
        ],
        compiler_params=pltpu.CompilerParams(collective_id=3, has_side_effects=True),
    )(partial, packed, grad_pre, weights)
    return summed.astype(jnp.float32), taps_sum.reshape(taps, channels)[: taps - 1], in_grad


def padded_2(cells, sides, width):
    for axis, dim in sides:
        count = lax.axis_size(axis)
        ends = count - 1
        head = lax.slice_in_dim(cells, 0, width, axis=dim)
        tail = lax.slice_in_dim(cells, cells.shape[dim] - width, cells.shape[dim], axis=dim)
        cells = jnp.concatenate(
            [
                lax.ppermute(tail, axis, [(i, (i + 1) % count) for i in range(ends)]),
                cells,
                lax.ppermute(head, axis, [((i + 1) % count, i) for i in range(ends)]),
            ],
            axis=dim,
        )
    return cells


def restore(quantized, scales):
    per_channel = jnp.repeat(scales.T, 128, axis=1)
    return (quantized.astype(jnp.float32) * per_channel).astype(jnp.bfloat16)


def depthwise(padded, kernel, frames):
    running = jnp.zeros((frames, padded.shape[1]), jnp.float32)
    for offset in range(kernel.shape[0]):
        running = running + kernel[offset] * padded[offset : offset + frames].astype(jnp.float32)
    return running


def plain(
    saved_codes, code_scales, lengths, in_weight, conv_kernel, bn_gain, bn_shift, out_grad
):
    frames = saved_codes.shape[1]
    feature_width = saved_codes.shape[2]
    tap_count = conv_kernel.shape[0]
    half_span = (tap_count - 1) // 2
    groups = lengths.shape[0]
    group_at = lax.axis_index("dp")
    length = jnp.sum(jnp.where(jnp.arange(groups, dtype=jnp.int32) == group_at, lengths, 0))
    counted = jnp.sum(lengths).astype(jnp.float32)
    first_frame = lax.axis_index("seq") * frames
    valid_mask = (first_frame + jnp.arange(frames, dtype=jnp.int32) < length).astype(jnp.float32)[
        :, None
    ]
    restored = restore(saved_codes[0], code_scales[0])
    weights = lax.all_gather(in_weight, "dp", axis=0, tiled=True)
    pre_act = lax.dot_general(
        restored, weights, (((1,), (1,)), ((), ())), preferred_element_type=jnp.float32
    )
    linear = pre_act[:, :feature_width]
    gate_part = jax.nn.sigmoid(pre_act[:, feature_width:])
    gated = (linear * gate_part * valid_mask).astype(jnp.bfloat16)
    gated_pad = padded_2(gated, (("seq", 0),), half_span)
    conv_out = depthwise(gated_pad, conv_kernel, frames)
    mean_value = lax.psum(jnp.sum(conv_out * valid_mask, axis=0), ("dp", "seq")) / counted
    centered = (conv_out - mean_value) * valid_mask
    variance = lax.psum(jnp.sum(centered * centered, axis=0), ("dp", "seq")) / counted
    inverse = lax.rsqrt(variance + EPS)
    normed = (conv_out - mean_value) * inverse
    shaped = bn_gain * normed + bn_shift
    smooth = jax.nn.sigmoid(shaped)
    grad_shaped = (
        out_grad[0].astype(jnp.float32) * valid_mask * smooth * (1.0 + shaped * (1.0 - smooth))
    )
    shift_grad, gain_grad = lax.psum(
        (jnp.sum(grad_shaped, axis=0), jnp.sum(grad_shaped * normed, axis=0)), ("dp", "seq")
    )
    grad_conv = (
        bn_gain * inverse * (grad_shaped - (shift_grad + normed * gain_grad) / counted) * valid_mask
    )
    kernel_part = jnp.stack(
        [
            jnp.sum(grad_conv * gated_pad[offset : offset + frames].astype(jnp.float32), axis=0)
            for offset in range(tap_count)
        ]
    )
    kernel_grad = lax.psum(kernel_part, ("dp", "seq"))
    grad_pad = padded_2(grad_conv, (("seq", 0),), half_span)
    grad_gated = depthwise(grad_pad, conv_kernel[::-1], frames) * valid_mask
    grad_pre = jnp.concatenate(
        [grad_gated * gate_part, grad_gated * linear * gate_part * (1.0 - gate_part)], axis=1
    ).astype(jnp.bfloat16)
    in_grad = jnp.dot(grad_pre, weights, preferred_element_type=jnp.float32)
    own_columns = lax.all_to_all(grad_pre[None], "dp", split_axis=2, concat_axis=0, tiled=True)
    local_rows = lax.dot_general(
        own_columns,
        lax.all_gather(restored[None], "dp", axis=0, tiled=True),
        (((0, 1), (0, 1)), ((), ())),
        preferred_element_type=jnp.float32,
    )
    weight_grad = lax.psum(local_rows, "seq")
    return (in_grad.astype(jnp.bfloat16)[None], weight_grad, kernel_grad, gain_grad, shift_grad)


def per_device(
    saved_codes, code_scales, lengths, in_weight, conv_kernel, bn_gain, bn_shift, out_grad
):
    if lax.axis_size("dp") != 4 or lax.axis_size("seq") != 8:
        return plain(
            saved_codes, code_scales, lengths, in_weight, conv_kernel, bn_gain, bn_shift, out_grad
        )
    weights, x_all, x = gather_weights(in_weight, saved_codes[0], code_scales[0])
    pre_act = lax.dot_general(
        x, weights, (((1,), (1,)), ((), ())), preferred_element_type=jnp.float32
    )
    own_columns, kernel_part, gain_grad, shift_grad, grad_pre = middle(
        pre_act, lengths, conv_kernel, bn_gain, bn_shift, out_grad[0]
    )
    local_rows = lax.dot_general(
        own_columns, x_all, (((0, 1), (0, 1)), ((), ())), preferred_element_type=jnp.float32
    )
    part = weights.shape[0] // grad_pre.shape[0]
    weight_grad, kernel_grad, in_grad = sum_grads(
        local_rows, kernel_part, grad_pre, weights.reshape(-1, part, weights.shape[1])
    )
    return (
        in_grad[None], weight_grad, kernel_grad, gain_grad[0], shift_grad[0]
    )


def solution(mesh):
    in_specs = (
        P("dp", "seq", None),
        P("dp", None, "seq"),
        P(),
        P("dp", None),
        P(),
        P(),
        P(),
        P("dp", "seq", None),
    )
    out_specs = (P("dp", "seq", None), P("dp", None), P(), P(), P())
    return jax.shard_map(
        per_device, mesh=mesh, in_specs=in_specs, out_specs=out_specs, check_vma=False
    )
```
